1024 devices in a mesh: ctx: 32 (over z, x_lo), head: 32 (over x_hi, y, core).
Axes of the slice: x: 8 (x_hi: 2, x_lo: 4; x = x_hi * 4 + x_lo), y: 8, z: 8, core: 2. Of those that a mesh axis runs over, the one named last changes fastest.
Arguments:
- compressed: bfloat16 [8192, 576], P('ctx'), may hold values from -6 to 6
- query: bfloat16 [8192, 24576], P('ctx', 'head'), may hold values from -6 to 6
- out_grad: bfloat16 [8192, 16384], P('ctx', 'head'), may hold values from -6 to 6
- up_weight: bfloat16 [512, 32768], P(None, 'head'), may hold values from -0.25 to 0.25
- lengths: int32 [96], replicated, may hold values from 1 to 256, 8192 in all
Outputs:
- grad_query: bfloat16 [8192, 24576], P('ctx', 'head')
- grad_compressed: float32 [8192, 576], P(('ctx', 'head'))
- grad_up_weight: float32 [512, 32768], P('ctx', 'head')
The draws below stay inside these ranges and needn't reach their ends.
Inputs may be any that keep to these rules, and one draw needn't show every extreme that they name: The lengths sum to 8192; the longest document has exactly 256 tokens.
All inputs are finite; a program needn't handle non-finite values.
Results may differ from the reference program's by a relative error of at most 0.025.
Values may be sent and summed in bfloat16 or wider, within the bound.
No kernel may reach another device: no remote copies, remote signals or barrier semaphores. Data moves between devices by JAX's collectives and lax.ppermute only.
A program may use at most 32 MiB of HBM per device.

```python
import math
import jax
import jax.numpy as jnp
import numpy as np
from jax import lax

LATENT = 512
ROPE = 64
NOPE = 128
VDIM = 128
HEADS = 128
TOK_DEV = 256
SEQ = 8192
NDOC = 96
N_CTX = 32


def level_of(own_key, dims, cuts, low, high):
    gain = 1.0
    for axis_at, parts in cuts:
        heights = jax.random.uniform(jax.random.fold_in(jax.random.fold_in(own_key, 6), axis_at), (parts,), jnp.float32, low / len(cuts), high / len(cuts))
        gain = gain * jnp.repeat(jnp.exp(heights), dims[axis_at] // parts).reshape((-1,) + (1,) * (len(dims) - 1 - axis_at))
    return gain


def length_profile(number_of, total, most, lean):
    weights = [(1 << 20) // math.isqrt(rank ** lean) + 1 for rank in range(2, number_of + 1)]
    spare, given = total - most - (number_of - 1), [1] * (number_of - 1)
    while spare > 0:
        free = [i for i in range(number_of - 1) if given[i] < most]
        whole, budget = sum([weights[i] for i in free]), spare
        for i in free:
            extra = min(most - given[i], max(1, budget * weights[i] // whole), spare)
            given[i] = given[i] + extra
            spare = spare - extra
    return np.array([most] + given)


def uneven(key, count, total, reach, skew):
    if count == 2:
        one = jax.random.randint(key, (), max(1, total - reach), min(reach, total - 1) + 1)
        return jnp.stack([one, total - one])
    sizes = jnp.asarray(length_profile(count, total, reach, skew), jnp.int32)
    pairs = (count - 1) // 2
    giver, sink = sizes[1:1 + 2 * pairs:2], sizes[2:2 + 2 * pairs:2]
    slack = jnp.minimum(giver - 1, reach - sink)
    shifted = jax.random.randint(jax.random.fold_in(key, 1), (pairs,), 0, 1 << 20) % (slack + 1)
    sizes = sizes.at[1:1 + 2 * pairs:2].set(giver - shifted).at[2:2 + 2 * pairs:2].set(sink + shifted)
    return sizes[jax.random.permutation(jax.random.fold_in(key, 2), count)]


def noise(rng, extent, scale, limit, cuts=(), held_as=jnp.bfloat16):
    entries = jax.random.normal(rng, extent, jnp.float32) * scale
    if len(cuts) > 0:
        entries = level_of(rng, extent, cuts, -0.22, 0.18) * entries
    return jnp.clip(entries, min=-limit, max=limit).astype(held_as)


def setup_inputs(seed: int = 0) -> dict:
    seeds = jax.random.split(jax.random.key(seed), 6)
    return {
        "compressed": noise(seeds[0], (SEQ, LATENT + ROPE), 1.0, 6.0, ((0, 32),)),
        "query": noise(seeds[1], (SEQ, HEADS * (NOPE + ROPE)), 1.0, 6.0, ((0, 32), (1, 32))),
        "out_grad": noise(seeds[2], (SEQ, HEADS * VDIM), 1.0, 6.0, ((0, 32), (1, 32))),
        "up_weight": noise(seeds[3], (LATENT, HEADS * (NOPE + VDIM)), LATENT ** -0.5, 0.25, ((1, 32),)),
        "lengths": uneven(seeds[4], NDOC, SEQ, TOK_DEV, 2).astype(jnp.int32),
    }


def widen(values):
    return values.astype(jnp.float32)

def reference(compressed, query, out_grad, up_weight, lengths):
    head_width = NOPE + ROPE
    pair_width = NOPE + VDIM
    scaling = 1.0 / math.sqrt(head_width)
    ends = jnp.cumsum(lengths).astype(jnp.int32)
    positions = jnp.arange(SEQ, dtype=jnp.int32)
    doc_start = lax.optimization_barrier(jnp.sum(jnp.where(ends[None, :] <= positions[:, None], lengths[None, :], 0), axis=1)).astype(jnp.int32)
    padded = jnp.concatenate([jnp.zeros((TOK_DEV, LATENT + ROPE), compressed.dtype), compressed], axis=0)

    def block_step(carry, block):
        weight_acc, latent_acc = carry
        first = (block * TOK_DEV).astype(jnp.int32)
        queries = lax.dynamic_slice_in_dim(query, first, TOK_DEV, 0).reshape(TOK_DEV, HEADS, head_width)
        grads_out = lax.dynamic_slice_in_dim(out_grad, first, TOK_DEV, 0).reshape(TOK_DEV, HEADS, VDIM)
        window = lax.dynamic_slice_in_dim(padded, first, 2 * TOK_DEV, 0)
        keys_values = jnp.dot(window[:, :LATENT], up_weight, preferred_element_type=jnp.float32)
        keys_values = keys_values.astype(jnp.bfloat16).reshape(2 * TOK_DEV, HEADS, pair_width)
        key_nope = keys_values[:, :, :NOPE]
        values = keys_values[:, :, NOPE:]
        key_rope = window[:, LATENT:]
        query_nope = queries[:, :, :NOPE]
        query_rope = queries[:, :, NOPE:]
        query_pos = first + jnp.arange(TOK_DEV, dtype=jnp.int32)
        key_pos = first - TOK_DEV + jnp.arange(2 * TOK_DEV, dtype=jnp.int32)
        query_start = lax.dynamic_slice_in_dim(doc_start, first, TOK_DEV, 0)
        visible = (key_pos[None, :] >= query_start[:, None]) & (key_pos[None, :] <= query_pos[:, None])
        scores = (jnp.einsum('thd,shd->hts', widen(query_nope), widen(key_nope)) + jnp.einsum('thd,sd->hts', widen(query_rope), widen(key_rope))) * scaling
        weights = jnp.where(visible[None], jnp.exp(scores), 0.0)
        probs = weights / lax.optimization_barrier(jnp.sum(weights, axis=-1, keepdims=True))
        probs_b = probs.astype(jnp.bfloat16)
        attended = jnp.einsum('hts,shd->thd', widen(probs_b), widen(values)).astype(jnp.bfloat16)
        delta = lax.optimization_barrier(jnp.sum(widen(grads_out) * widen(attended), axis=-1))
        prob_grad = jnp.einsum('thd,shd->hts', widen(grads_out), widen(values))
        score_grad = (probs * (prob_grad - jnp.transpose(delta)[:, :, None]) * scaling).astype(jnp.bfloat16)
        grad_nope = jnp.einsum('hts,shd->thd', widen(score_grad), widen(key_nope))
        grad_rope = jnp.einsum('hts,sd->thd', widen(score_grad), widen(key_rope))
        grad_q = jnp.concatenate([grad_nope, grad_rope], axis=-1).reshape(TOK_DEV, HEADS * head_width).astype(jnp.bfloat16)
        key_grad = jnp.einsum('hts,thd->shd', widen(score_grad), widen(query_nope))
        rope_grad = jnp.einsum('hts,thd->sd', widen(score_grad), widen(query_rope))
        value_grad = jnp.einsum('hts,thd->shd', widen(probs_b), widen(grads_out))
        kv_grads = jnp.concatenate([key_grad, value_grad], axis=-1).reshape(2 * TOK_DEV, HEADS * pair_width).astype(jnp.bfloat16)
        weight_acc = weight_acc + jnp.dot(jnp.transpose(window[:, :LATENT]), kv_grads, preferred_element_type=jnp.float32)
        latent_part = jnp.dot(kv_grads, jnp.transpose(up_weight), preferred_element_type=jnp.float32)
        contribution = jnp.concatenate([latent_part, rope_grad], axis=1)
        current = lax.dynamic_slice_in_dim(latent_acc, first, 2 * TOK_DEV, 0)
        latent_acc = lax.dynamic_update_slice_in_dim(latent_acc, current + contribution, first, 0)
        return ((weight_acc, latent_acc), grad_q)
    start_carry = (jnp.zeros((LATENT, HEADS * pair_width), jnp.float32), jnp.zeros((SEQ + TOK_DEV, LATENT + ROPE), jnp.float32))
    (weight_acc, latent_acc), grad_blocks = lax.scan(block_step, start_carry, jnp.arange(N_CTX, dtype=jnp.int32))
    return (grad_blocks.reshape(SEQ, HEADS * head_width), latent_acc[TOK_DEV:], weight_acc)
```

```python
import math

import jax
import jax.numpy as jnp
from jax import lax
from jax.sharding import Mesh
from jax.sharding import PartitionSpec as P

LATENT = 512
ROPE = 64
NOPE = 128
VDIM = 128
CTX = ("zh", "z0", "x1", "x0")
HEAD = ("xh", "y", "core")
F32 = jnp.float32
BF16 = jnp.bfloat16


def ctx_shift(x, by):
    pairs = [(i, i + by) for i in range(32) if 0 <= i + by < 32]
    return lax.ppermute(x, CTX, pairs)


def quad_partner(x, dz, dx):
    pairs = [(i, i ^ (4 * dz) ^ dx) for i in range(32)]
    return lax.ppermute(x, CTX, pairs)


def attention_grads(own, prev, query, out_grad, up_weight, lengths, ctx_rank):
    tok = own.shape[0]
    width = NOPE + ROPE
    heads = query.shape[1] // width
    scaling = 1.0 / math.sqrt(width)
    first_pos = ctx_rank * tok
    ends = jnp.cumsum(lengths)
    query_pos = first_pos + jnp.arange(tok, dtype=jnp.int32)
    key_pos = first_pos - tok + jnp.arange(2 * tok, dtype=jnp.int32)
    start = jnp.sum(jnp.where(ends[None, :] <= query_pos[:, None], lengths[None, :], 0), axis=1)
    visible = (key_pos[None, :] >= start[:, None]) & (key_pos[None, :] <= query_pos[:, None])
    window = jnp.concatenate([prev, own], axis=0)
    kv = jnp.dot(window[:, :LATENT], up_weight, preferred_element_type=F32).astype(BF16)
    kv = kv.reshape(2 * tok, heads, NOPE + VDIM)
    k, v = kv[:, :, :NOPE], kv[:, :, NOPE:]
    kr = window[:, LATENT:]
    q = query.reshape(tok, heads, width)
    qn, qr = q[:, :, :NOPE], q[:, :, NOPE:]
    do = out_grad.reshape(tok, heads, VDIM)
    scores = (
        jnp.einsum("thd,shd->hts", qn, k, preferred_element_type=F32)
        + jnp.einsum("thd,sd->hts", qr, kr, preferred_element_type=F32)
    ) * scaling
    weights = jnp.where(visible[None], jnp.exp(scores), 0.0)
    probs = weights / jnp.sum(weights, axis=-1, keepdims=True)
    probs_b = probs.astype(BF16)
    attended = jnp.einsum("hts,shd->thd", probs_b, v, preferred_element_type=F32).astype(BF16)
    delta = jnp.sum(do.astype(F32) * attended.astype(F32), axis=-1)
    dp = jnp.einsum("thd,shd->hts", do, v, preferred_element_type=F32)
    ds = (probs * (dp - jnp.transpose(delta)[:, :, None]) * scaling).astype(BF16)
    dqn = jnp.einsum("hts,shd->thd", ds, k, preferred_element_type=F32)
    dqr = jnp.einsum("hts,sd->thd", ds, kr, preferred_element_type=F32)
    dq = jnp.concatenate([dqn, dqr], axis=-1).reshape(tok, heads * width).astype(BF16)
    dk = jnp.einsum("hts,thd->shd", ds, qn, preferred_element_type=F32)
    dr = jnp.einsum("hts,thd->sd", ds, qr, preferred_element_type=F32)
    dv = jnp.einsum("hts,thd->shd", probs_b, do, preferred_element_type=F32)
    dkv = jnp.concatenate([dk, dv], axis=-1).reshape(2 * tok, heads * (NOPE + VDIM)).astype(BF16)
    return dq, dkv, dr, window


def body(compressed, query, out_grad, up_weight, lengths):
    ctx_rank = lax.axis_index(CTX)
    core = lax.axis_index("core")
    z0, x0 = lax.axis_index("z0"), lax.axis_index("x0")
    prev = ctx_shift(compressed, 1)
    dq, dkv, dr, window = attention_grads(
        compressed, prev, query, out_grad, up_weight, lengths, ctx_rank
    )

    latent = jnp.einsum("sk,lk->sl", dkv, up_weight, preferred_element_type=F32)
    total = jnp.concatenate([latent, dr], axis=1).reshape(2, 16, 2, 8, LATENT + ROPE)
    mine = lax.dynamic_index_in_dim(total, core, 2, keepdims=False)
    theirs = lax.dynamic_index_in_dim(total, 1 - core, 2, keepdims=False).astype(BF16)
    got = lax.ppermute(theirs, "core", [(0, 1), (1, 0)])
    pair = mine + got.astype(F32)
    back = ctx_shift(pair[0].astype(BF16), -1)
    part = (pair[1] + back.astype(F32)).astype(BF16)

    cols = window[:, :LATENT].reshape(512, 4, 2, 2, 2, 16)

    def piece(a, b):
        sel = lax.dynamic_index_in_dim(cols, a, 2, keepdims=False)
        sel = lax.dynamic_index_in_dim(sel, b, 3, keepdims=False).reshape(512, 128)
        return jnp.einsum("sl,sk->lk", sel, dkv, preferred_element_type=F32)

    got_x = quad_partner(piece(z0, 1 - x0).astype(BF16), 0, 1)
    got_z = quad_partner(piece(1 - z0, x0).astype(BF16), 1, 0)
    got_d = quad_partner(piece(1 - z0, 1 - x0).astype(BF16), 1, 1)
    quad = piece(z0, x0) + got_x.astype(F32) + got_z.astype(F32) + got_d.astype(F32)

    parts = lax.all_to_all(part, ("xh", "y"), 0, 0)
    grad_compressed = jnp.sum(parts.astype(F32), axis=0)
    eighths = lax.all_to_all(quad.astype(BF16).reshape(8, 16, -1), ("zh", "x1"), 0, 0)
    grad_weight = jnp.sum(eighths.astype(F32), axis=0)
    return dq, grad_compressed, grad_weight


def solution(mesh):
    fine = Mesh(
        mesh.devices.reshape(4, 2, 2, 2, 2, 8, 2), ("zh", "z0", "x1", "x0", "xh", "y", "core")
    )
    placed = (P(CTX, None), P(CTX, HEAD), P(CTX, HEAD), P(None, HEAD), P())
    return jax.shard_map(
        body,
        mesh=fine,
        in_specs=placed,
        out_specs=(P(CTX, HEAD), P(CTX + HEAD, None), P(CTX, HEAD)),
        check_vma=False,
    )
```

```python
import math

import jax
import jax.numpy as jnp
from jax import lax
from jax.experimental import pallas as pl
from jax.experimental.pallas import tpu as pltpu
from jax.sharding import Mesh
from jax.sharding import PartitionSpec as P


LATENT = 512
ROPE = 64
NOPE = 128
VDIM = 128
HEADS = 4
TOK = 256
PAIR = NOPE + VDIM
WIDTH = NOPE + ROPE
SCALING = 1.0 / math.sqrt(WIDTH)
CTX = ("zh", "z0", "x1", "x0")
HEAD = ("xh", "y", "core")
F32 = jnp.float32
BF16 = jnp.bfloat16
NT = (((1,), (1,)), ((), ()))
TN = (((0,), (0,)), ((), ()))
VMEM = pl.BlockSpec(memory_space=pltpu.VMEM)
SMEM = pl.BlockSpec(memory_space=pltpu.SMEM)


def dot(a, b, dims=(((1,), (0,)), ((), ()))):
    return lax.dot_general(a, b, dims, preferred_element_type=F32)


def ctx_shift(x, by):
    pairs = [(i, i + by) for i in range(32) if 0 <= i + by < 32]
    return lax.ppermute(x, CTX, pairs)


def iota(shape, dim):
    return lax.broadcasted_iota(jnp.int32, shape, dim)


def keys_and_values(xt_ref, w_ref, ke_ref):
    kv = dot(xt_ref[:LATENT, :], w_ref[...], TN).astype(BF16)
    rope = jnp.concatenate([xt_ref[LATENT:, :].astype(F32), jnp.zeros((ROPE, TOK), F32)], axis=0)
    rope = jnp.transpose(rope).astype(BF16)
    values = []
    for h in range(HEADS):
        ke_ref[h, :, :NOPE] = kv[:, h * PAIR : h * PAIR + NOPE]
        ke_ref[h, :, NOPE:] = rope
        values.append(kv[:, h * PAIR + NOPE : (h + 1) * PAIR])
    return values


def own_kernel(start_ref, xt_ref, q_ref, do_ref, w_ref, ke_ref, qe_ref, e_ref, dp_ref, lg_ref):
    lane = iota((TOK, 256), 1)
    for h in range(HEADS):
        base = (h // 2) * 2 * WIDTH
        if h % 2 == 0:
            rows = q_ref[:, base : base + 256].astype(F32)
        else:
            rows = pltpu.roll(q_ref[:, base + 128 : base + 384].astype(F32), 192, 1)
        qe_ref[h] = jnp.where(lane < WIDTH, rows, 0.0).astype(BF16)
    values = keys_and_values(xt_ref, w_ref, ke_ref)
    key = iota((TOK, TOK), 0)
    seen = (key >= start_ref[...]) & (key <= iota((TOK, TOK), 1))
    for h in range(HEADS):
        scores = dot(ke_ref[h], qe_ref[h], NT) * SCALING
        e = jnp.where(seen, jnp.exp(scores), 0.0)
        dp = dot(values[h], do_ref[:, h * VDIM : (h + 1) * VDIM], NT)
        e_ref[h] = e
        dp_ref[h] = dp
        lg_ref[h : h + 1, :] = jnp.sum(e, axis=0, keepdims=True)
        lg_ref[h + 4 : h + 5, :] = jnp.sum(e * dp, axis=0, keepdims=True)


def chosen_rows(xt_ref, bit):
    return jnp.concatenate(
        [xt_ref[pl.ds(pl.multiple_of((2 * i + bit) * 64, 64), 64), :] for i in range(4)], axis=0
    )


def weight_half(own_ref, prev_ref, bit, dkv_ref):
    half = dot(chosen_rows(prev_ref, bit), dkv_ref[0])
    return half + dot(chosen_rows(own_ref, bit), dkv_ref[1])


def window_kernel(
    z0_ref, start_ref, xt_ref, own_ref, qe_ref, do_ref, w_ref, e_ref, dp_ref, lg_ref,
    ke_ref, ds_ref, dkv_ref, lat_ref, theirs_ref,
):
    values = keys_and_values(xt_ref, w_ref, ke_ref)
    seen = iota((TOK, TOK), 0) - TOK >= start_ref[...]
    rope_grads = [jnp.zeros((TOK, 128), F32), jnp.zeros((TOK, 128), F32)]
    for h in range(HEADS):
        qe = qe_ref[h]
        do = do_ref[:, h * VDIM : (h + 1) * VDIM]
        scores = dot(ke_ref[h], qe, NT) * SCALING
        e = jnp.where(seen, jnp.exp(scores), 0.0)
        dp = dot(values[h], do, NT)
        norm = 1.0 / (lg_ref[h : h + 1, :] + jnp.sum(e, axis=0, keepdims=True))
        delta = (lg_ref[h + 4 : h + 5, :] + jnp.sum(e * dp, axis=0, keepdims=True)) * norm
        for half in range(2):
            if half == 1:
                e, dp = e_ref[h], dp_ref[h]
            probs = e * norm
            ds = (probs * (dp - delta) * SCALING).astype(BF16)
            ds_ref[h, half] = ds
            dk = dot(ds, qe)
            dkv_ref[half, :, h * PAIR : h * PAIR + NOPE] = dk[:, :NOPE].astype(BF16)
            rope_grads[half] = rope_grads[half] + dk[:, NOPE:]
            dkv_ref[half, :, h * PAIR + NOPE : (h + 1) * PAIR] = dot(
                probs.astype(BF16), do
            ).astype(BF16)
    theirs_ref[...] = weight_half(own_ref, xt_ref, 1 - z0_ref[0], dkv_ref).astype(BF16)
    lat_ref[:, :LATENT] = dot(dkv_ref[1], w_ref[...], NT).astype(BF16)
    lat_ref[:, LATENT : 2 * LATENT] = dot(dkv_ref[0], w_ref[...], NT).astype(BF16)
    lat_ref[:, 2 * LATENT :] = (rope_grads[1] + pltpu.roll(rope_grads[0], ROPE, 1)).astype(BF16)


def rest_kernel(z0_ref, xt_ref, own_ref, kep_ref, keo_ref, ds_ref, dkv_ref, dq_ref, mine_ref):
    for pair in range(HEADS // 2):
        parts = []
        for h in (2 * pair, 2 * pair + 1):
            parts.append(dot(ds_ref[h, 0], kep_ref[h], TN) + dot(ds_ref[h, 1], keo_ref[h], TN))
        moved = pltpu.roll(parts[1], ROPE, 1)
        base = pair * 2 * WIDTH
        dq_ref[:, base : base + 128] = parts[0][:, :128].astype(BF16)
        dq_ref[:, base + 128 : base + 256] = (parts[0][:, 128:] + moved[:, :128]).astype(BF16)
        dq_ref[:, base + 256 : base + 384] = moved[:, 128:].astype(BF16)
    mine_ref[...] = weight_half(own_ref, xt_ref, z0_ref[0], dkv_ref)


def call(kernel, outs, scalars, flops, *args):
    specs = [SMEM] * scalars + [VMEM] * (len(args) - scalars)
    return pl.pallas_call(
        kernel,
        out_shape=[jax.ShapeDtypeStruct(s, d) for s, d in outs],
        in_specs=specs,
        out_specs=[VMEM] * len(outs),
        compiler_params=pltpu.CompilerParams(vmem_limit_bytes=20 << 20),
        cost_estimate=pl.CostEstimate(flops=flops, bytes_accessed=4 << 20, transcendentals=0),
    )(*args)


def attend(own, prev, query, out_grad, up_weight, start, z0):
    square = (HEADS, TOK, 256)
    keo, qe, e, dp, lg = call(
        own_kernel,
        [(square, BF16), (square, BF16), (square, F32), (square, F32), ((8, TOK), F32)],
        0, 470_000_000, start, own, query, out_grad, up_weight,
    )
    kep, ds, dkv, latent, theirs = call(
        window_kernel,
        [
            (square, BF16),
            ((HEADS, 2, TOK, TOK), BF16),
            ((2, TOK, HEADS * PAIR), BF16),
            ((TOK, 2 * LATENT + 2 * ROPE), BF16),
            ((TOK, HEADS * PAIR), BF16),
        ],
        1, 1_700_000_000, z0, start, prev, own, qe, out_grad, up_weight, e, dp, lg,
    )
    return latent, theirs, (prev, own, kep, keo, ds, dkv)


def finish(z0, saved):
    return call(
        rest_kernel,
        [((TOK, HEADS * WIDTH), BF16), ((TOK, HEADS * PAIR), F32)],
        1, 540_000_000, z0, *saved,
    )


def body(compressed, query, out_grad, up_weight, lengths):
    ctx_rank = lax.axis_index(CTX)
    z0 = lax.axis_index("z0").reshape(1)
    own = compressed.T
    prev = ctx_shift(own, 1)

    first_pos = ctx_rank * TOK
    ends = jnp.cumsum(lengths)
    query_pos = first_pos + jnp.arange(TOK, dtype=jnp.int32)
    start = jnp.sum(jnp.where(ends[:, None] <= query_pos[None, :], lengths[:, None], 0), axis=0)
    start = (start - first_pos)[None, :]

    latent, theirs, saved = attend(own, prev, query, out_grad, up_weight, start, z0)
    got = lax.ppermute(theirs, CTX, [(i, i ^ 4) for i in range(32)])
    parts = lax.all_to_all(latent.reshape(32, 8, -1), HEAD, 0, 0)
    dq, mine = finish(z0, saved)
    both = (mine + got.astype(F32)).astype(BF16).reshape(16, 16, -1)
    sixteenths = lax.all_to_all(both, ("zh", "x1", "x0"), 0, 0)
    summed = jnp.sum(parts.astype(F32), axis=0)
    kept = jnp.concatenate([summed[:, :LATENT], summed[:, 2 * LATENT : 2 * LATENT + ROPE]], axis=1)
    sent = jnp.concatenate([summed[:, LATENT : 2 * LATENT], summed[:, 2 * LATENT + ROPE :]], axis=1)
    grad_compressed = kept + ctx_shift(sent, -1)
    grad_weight = jnp.sum(sixteenths.astype(F32), axis=0)
    return dq, grad_compressed, grad_weight


def solution(mesh):
    fine = Mesh(
        mesh.devices.reshape(4, 2, 2, 2, 2, 8, 2), ("zh", "z0", "x1", "x0", "xh", "y", "core")
    )
    placed = (P(CTX, None), P(CTX, HEAD), P(CTX, HEAD), P(None, HEAD), P())
    return jax.shard_map(
        body,
        mesh=fine,
        in_specs=placed,
        out_specs=(P(CTX, HEAD), P(CTX + HEAD, None), P(CTX, HEAD)),
        check_vma=False,
    )
```

```python
import math

import jax
import jax.numpy as jnp
from jax import lax
from jax.experimental import pallas as pl
from jax.experimental.pallas import tpu as pltpu
from jax.sharding import Mesh
from jax.sharding import PartitionSpec as P


LATENT = 512
ROPE = 64
NOPE = 128
VDIM = 128
HEADS = 4
TOK = 256
PAIR = NOPE + VDIM
WIDTH = NOPE + ROPE
SCALING = 1.0 / math.sqrt(WIDTH)
CTX = ("z2", "z1", "z0", "x1", "x0")
HEAD = ("xh", "y", "core")
F32 = jnp.float32
BF16 = jnp.bfloat16
NT = (((1,), (1,)), ((), ()))
TN = (((0,), (0,)), ((), ()))
VMEM = pl.BlockSpec(memory_space=pltpu.VMEM)
SMEM = pl.BlockSpec(memory_space=pltpu.SMEM)


def dot(a, b, dims=(((1,), (0,)), ((), ()))):
    return lax.dot_general(a, b, dims, preferred_element_type=F32)


def ctx_shift(x, by):
    pairs = [(i, i + by) for i in range(32) if 0 <= i + by < 32]
    return lax.ppermute(x, CTX, pairs)


def iota(shape, dim):
    return lax.broadcasted_iota(jnp.int32, shape, dim)


def keys_and_values(xt_ref, w_ref, ke_ref):
    kv = dot(xt_ref[:LATENT, :], w_ref[...], TN).astype(BF16)
    rope = jnp.concatenate([xt_ref[LATENT:, :].astype(F32), jnp.zeros((ROPE, TOK), F32)], axis=0)
    rope = jnp.transpose(rope).astype(BF16)
    values = []
    for h in range(HEADS):
        ke_ref[h, :, :NOPE] = kv[:, h * PAIR : h * PAIR + NOPE]
        ke_ref[h, :, NOPE:] = rope
        values.append(kv[:, h * PAIR + NOPE : (h + 1) * PAIR])
    return values


def own_kernel(start_ref, xt_ref, q_ref, do_ref, w_ref, ke_ref, qe_ref, e_ref, dp_ref, lg_ref):
    lane = iota((TOK, 256), 1)
    for h in range(HEADS):
        base = (h // 2) * 2 * WIDTH
        if h % 2 == 0:
            rows = q_ref[:, base : base + 256].astype(F32)
        else:
            rows = pltpu.roll(q_ref[:, base + 128 : base + 384].astype(F32), 192, 1)
        qe_ref[h] = jnp.where(lane < WIDTH, rows, 0.0).astype(BF16)
    values = keys_and_values(xt_ref, w_ref, ke_ref)
    key = iota((TOK, TOK), 0)
    seen = (key >= start_ref[...]) & (key <= iota((TOK, TOK), 1))
    for h in range(HEADS):
        scores = dot(ke_ref[h], qe_ref[h], NT) * SCALING
        e = jnp.where(seen, jnp.exp(scores), 0.0)
        dp = dot(values[h], do_ref[:, h * VDIM : (h + 1) * VDIM], NT)
        e_ref[h] = e
        dp_ref[h] = dp
        lg_ref[h : h + 1, :] = jnp.sum(e, axis=0, keepdims=True)
        lg_ref[h + 4 : h + 5, :] = jnp.sum(e * dp, axis=0, keepdims=True)


def piece_rows(xt_ref, z0, x0):
    rows = []
    for i in range(8):
        chunk = (((i // 2) * 2 + z0) * 2 + i % 2) * 2 + x0
        rows.append(xt_ref[pl.ds(pl.multiple_of(chunk * 16, 16), 16), :])
    return jnp.concatenate(rows, axis=0)


def weight_piece(own_ref, prev_ref, z0, x0, dkv_ref):
    part = dot(piece_rows(prev_ref, z0, x0), dkv_ref[0])
    return part + dot(piece_rows(own_ref, z0, x0), dkv_ref[1])


def window_kernel(
    bits_ref, start_ref, xt_ref, own_ref, qe_ref, do_ref, w_ref, e_ref, dp_ref, lg_ref,
    ke_ref, ds_ref, lat_ref, mine_ref, px_ref, pz_ref, pd_ref, dkv_ref,
):
    values = keys_and_values(xt_ref, w_ref, ke_ref)
    seen = iota((TOK, TOK), 0) - TOK >= start_ref[...]
    rope_grads = [jnp.zeros((TOK, 128), F32), jnp.zeros((TOK, 128), F32)]
    for h in range(HEADS):
        qe = qe_ref[h]
        do = do_ref[:, h * VDIM : (h + 1) * VDIM]
        scores = dot(ke_ref[h], qe, NT) * SCALING
        e = jnp.where(seen, jnp.exp(scores), 0.0)
        dp = dot(values[h], do, NT)
        norm = 1.0 / (lg_ref[h : h + 1, :] + jnp.sum(e, axis=0, keepdims=True))
        delta = (lg_ref[h + 4 : h + 5, :] + jnp.sum(e * dp, axis=0, keepdims=True)) * norm
        for half in range(2):
            if half == 1:
                e, dp = e_ref[h], dp_ref[h]
            probs = e * norm
            ds = (probs * (dp - delta) * SCALING).astype(BF16)
            ds_ref[h, half] = ds
            dk = dot(ds, qe)
            dkv_ref[half, :, h * PAIR : h * PAIR + NOPE] = dk[:, :NOPE].astype(BF16)
            rope_grads[half] = rope_grads[half] + dk[:, NOPE:]
            dkv_ref[half, :, h * PAIR + NOPE : (h + 1) * PAIR] = dot(
                probs.astype(BF16), do
            ).astype(BF16)
    z0, x0 = bits_ref[2], bits_ref[4]
    px_ref[...] = weight_piece(own_ref, xt_ref, z0, 1 - x0, dkv_ref).astype(BF16)
    pz_ref[...] = weight_piece(own_ref, xt_ref, 1 - z0, x0, dkv_ref).astype(BF16)
    pd_ref[...] = weight_piece(own_ref, xt_ref, 1 - z0, 1 - x0, dkv_ref).astype(BF16)
    mine_ref[...] = weight_piece(own_ref, xt_ref, z0, x0, dkv_ref)
    lat_ref[:, :LATENT] = dot(dkv_ref[1], w_ref[...], NT).astype(BF16)
    lat_ref[:, LATENT : 2 * LATENT] = dot(dkv_ref[0], w_ref[...], NT).astype(BF16)
    lat_ref[:, 2 * LATENT :] = (rope_grads[1] + pltpu.roll(rope_grads[0], ROPE, 1)).astype(BF16)


def query_kernel(kep_ref, keo_ref, ds_ref, dq_ref):
    for pair in range(HEADS // 2):
        parts = []
        for h in (2 * pair, 2 * pair + 1):
            parts.append(dot(ds_ref[h, 0], kep_ref[h], TN) + dot(ds_ref[h, 1], keo_ref[h], TN))
        moved = pltpu.roll(parts[1], ROPE, 1)
        base = pair * 2 * WIDTH
        dq_ref[:, base : base + 128] = parts[0][:, :128].astype(BF16)
        dq_ref[:, base + 128 : base + 256] = (parts[0][:, 128:] + moved[:, :128]).astype(BF16)
        dq_ref[:, base + 256 : base + 384] = moved[:, 128:].astype(BF16)


def quad_sum_kernel(bits_ref, mine_ref, gx_ref, gz_ref, gd_ref, kept_ref, px_ref, pz_ref, pd_ref, sum_ref):
    sum_ref[...] = (
        mine_ref[...] + gx_ref[...].astype(F32) + gz_ref[...].astype(F32) + gd_ref[...].astype(F32)
    )
    z1, x1 = bits_ref[1], bits_ref[3]
    for out_ref, z, x in (
        (kept_ref, z1, x1), (px_ref, z1, 1 - x1), (pz_ref, 1 - z1, x1), (pd_ref, 1 - z1, 1 - x1)
    ):
        for z2 in range(2):
            row = pl.multiple_of(((z2 * 2 + z) * 2 + x) * 16, 16)
            out_ref[z2 * 16 : z2 * 16 + 16, :] = sum_ref[pl.ds(row, 16), :].astype(out_ref.dtype)


def last_sum_kernel(bits_ref, mine_ref, gx_ref, gz_ref, gd_ref, kept_ref, sent_ref, sum_ref):
    sum_ref[...] = (
        mine_ref[...] + gx_ref[...].astype(F32) + gz_ref[...].astype(F32) + gd_ref[...].astype(F32)
    )
    z2 = bits_ref[0]
    kept_ref[...] = sum_ref[pl.ds(pl.multiple_of(z2 * 16, 16), 16), :]
    sent_ref[...] = sum_ref[pl.ds(pl.multiple_of((1 - z2) * 16, 16), 16), :].astype(BF16)


def call(kernel, outs, scalars, flops, *args, scratch=()):
    specs = [SMEM] * scalars + [VMEM] * (len(args) - scalars)
    return pl.pallas_call(
        kernel,
        out_shape=[jax.ShapeDtypeStruct(s, d) for s, d in outs],
        in_specs=specs,
        out_specs=[VMEM] * len(outs),
        scratch_shapes=list(scratch),
        compiler_params=pltpu.CompilerParams(vmem_limit_bytes=20 << 20),
        cost_estimate=pl.CostEstimate(flops=flops, bytes_accessed=4 << 20, transcendentals=0),
    )(*args)


def attend(own, prev, query, out_grad, up_weight, start, bits):
    square = (HEADS, TOK, 256)
    columns = HEADS * PAIR
    keo, qe, e, dp, lg = call(
        own_kernel,
        [(square, BF16), (square, BF16), (square, F32), (square, F32), ((8, TOK), F32)],
        0, 470_000_000, start, own, query, out_grad, up_weight,
    )
    kep, ds, latent, mine, *pieces = call(
        window_kernel,
        [
            (square, BF16),
            ((HEADS, 2, TOK, TOK), BF16),
            ((TOK, 2 * LATENT + 2 * ROPE), BF16),
            ((128, columns), F32),
            ((128, columns), BF16),
            ((128, columns), BF16),
            ((128, columns), BF16),
        ],
        1, 2_000_000_000, bits, start, prev, own, qe, out_grad, up_weight, e, dp, lg,
        scratch=[pltpu.VMEM((2, TOK, columns), BF16)],
    )
    return latent, mine, pieces, (kep, keo, ds)


def query_grad(saved):
    return call(query_kernel, [((TOK, HEADS * WIDTH), BF16)], 0, 270_000_000, *saved)[0]


def flip(x, mask):
    return lax.ppermute(x, CTX, [(i, i ^ mask) for i in range(32)])


def body(compressed, query, out_grad, up_weight, lengths):
    ctx_rank = lax.axis_index(CTX)
    bits = jnp.stack([lax.axis_index(name) for name in CTX]).astype(jnp.int32)
    own = compressed.T
    prev = ctx_shift(own, 1)

    first_pos = ctx_rank * TOK
    ends = jnp.cumsum(lengths)
    query_pos = first_pos + jnp.arange(TOK, dtype=jnp.int32)
    start = jnp.sum(jnp.where(ends[:, None] <= query_pos[None, :], lengths[:, None], 0), axis=0)
    start = (start - first_pos)[None, :]

    columns = HEADS * PAIR
    latent, mine, pieces, saved = attend(own, prev, query, out_grad, up_weight, start, bits)
    got_x = flip(pieces[0], 1)
    got_z = flip(pieces[1], 4)
    got_d = flip(pieces[2], 5)
    parts = lax.all_to_all(latent.reshape(32, 8, -1), HEAD, 0, 0)
    dq = query_grad(saved)
    kept, *sends = call(
        quad_sum_kernel,
        [((32, columns), F32)] + [((32, columns), BF16)] * 3,
        1, 1_000_000, bits, mine, got_x, got_z, got_d,
        scratch=[pltpu.VMEM((128, columns), F32)],
    )
    far_x = flip(sends[0], 2)
    far_z = flip(sends[1], 8)
    far_d = flip(sends[2], 10)
    last, sent = call(
        last_sum_kernel,
        [((16, columns), F32), ((16, columns), BF16)],
        1, 1_000_000, bits, kept, far_x, far_z, far_d,
        scratch=[pltpu.VMEM((32, columns), F32)],
    )
    grad_weight = last + flip(sent, 16).astype(F32)
    summed = jnp.sum(parts.astype(F32), axis=0)
    rope = 2 * LATENT + ROPE
    keep = jnp.concatenate([summed[:, :LATENT], summed[:, 2 * LATENT : rope]], axis=1)
    give = jnp.concatenate([summed[:, LATENT : 2 * LATENT], summed[:, rope:]], axis=1)
    grad_compressed = keep + ctx_shift(give, -1)
    return dq, grad_compressed, grad_weight


def solution(mesh):
    fine = Mesh(mesh.devices.reshape(2, 2, 2, 2, 2, 2, 8, 2), CTX + HEAD)
    placed = (P(CTX, None), P(CTX, HEAD), P(CTX, HEAD), P(None, HEAD), P())
    return jax.shard_map(
        body,
        mesh=fine,
        in_specs=placed,
        out_specs=(P(CTX, HEAD), P(CTX + HEAD, None), P(CTX, HEAD)),
        check_vma=False,
    )
```

```python
import math

import jax
import jax.numpy as jnp
from jax import lax
from jax.experimental import pallas as pl
from jax.experimental.pallas import tpu as pltpu
from jax.sharding import Mesh
from jax.sharding import PartitionSpec as P


LATENT = 512
ROPE = 64
NOPE = 128
VDIM = 128
HEADS = 4
TOK = 256
PAIR = NOPE + VDIM
WIDTH = NOPE + ROPE
SCALING = 1.0 / math.sqrt(WIDTH)
CTX = ("z2", "z1", "z0", "x1", "x0")
HEAD = ("xh", "y", "core")
F32 = jnp.float32
BF16 = jnp.bfloat16
NT = (((1,), (1,)), ((), ()))
TN = (((0,), (0,)), ((), ()))
VMEM = pl.BlockSpec(memory_space=pltpu.VMEM)


def dot(a, b, dims=(((1,), (0,)), ((), ()))):
    return lax.dot_general(a, b, dims, preferred_element_type=F32)


def ctx_shift(x, by):
    pairs = [(i, i + by) for i in range(32) if 0 <= i + by < 32]
    return lax.ppermute(x, CTX, pairs)


def iota(shape, dim):
    return lax.broadcasted_iota(jnp.int32, shape, dim)


def keys_and_values(xt_ref, w_ref, ke_ref):
    kv = dot(xt_ref[:LATENT, :], w_ref[...], TN).astype(BF16)
    rope = jnp.concatenate([xt_ref[LATENT:, :].astype(F32), jnp.zeros((ROPE, TOK), F32)], axis=0)
    rope = jnp.transpose(rope).astype(BF16)
    values = []
    for h in range(HEADS):
        ke_ref[h, :, :NOPE] = kv[:, h * PAIR : h * PAIR + NOPE]
        ke_ref[h, :, NOPE:] = rope
        values.append(kv[:, h * PAIR + NOPE : (h + 1) * PAIR])
    return values


def first_visible(len_ref):
    docs = len_ref.shape[1]
    lengths = jnp.broadcast_to(len_ref[...].astype(F32), (docs, docs))
    row, col = iota((docs, docs), 0), iota((docs, docs), 1)
    ends = jnp.sum(jnp.where(col <= row, lengths, 0.0), axis=1, keepdims=True)
    each = jnp.sum(jnp.where(col == row, lengths, 0.0), axis=1, keepdims=True)
    first = lax.axis_index(CTX) * TOK
    query = (iota((docs, TOK), 1) + first).astype(F32)
    before = jnp.sum(jnp.where(ends <= query, each, 0.0), axis=0, keepdims=True)
    return before.astype(jnp.int32) - first


def own_kernel(
    len_ref, xt_ref, q_ref, do_ref, w_ref, ke_ref, qe_ref, e_ref, dp_ref, lg_ref, start_ref
):
    start_ref[...] = first_visible(len_ref)
    lane = iota((TOK, 256), 1)
    for h in range(HEADS):
        base = (h // 2) * 2 * WIDTH
        if h % 2 == 0:
            rows = q_ref[:, base : base + 256].astype(F32)
        else:
            rows = pltpu.roll(q_ref[:, base + 128 : base + 384].astype(F32), 192, 1)
        qe_ref[h] = jnp.where(lane < WIDTH, rows, 0.0).astype(BF16)
    values = keys_and_values(xt_ref, w_ref, ke_ref)
    key = iota((TOK, TOK), 0)
    seen = (key >= start_ref[...]) & (key <= iota((TOK, TOK), 1))
    for h in range(HEADS):
        scores = dot(ke_ref[h], qe_ref[h], NT) * SCALING
        e = jnp.where(seen, jnp.exp(scores), 0.0)
        dp = dot(values[h], do_ref[:, h * VDIM : (h + 1) * VDIM], NT)
        e_ref[h] = e
        dp_ref[h] = dp
        lg_ref[h : h + 1, :] = jnp.sum(e, axis=0, keepdims=True)
        lg_ref[h + 4 : h + 5, :] = jnp.sum(e * dp, axis=0, keepdims=True)


def rows_of(xt_ref, z0=None, x0=None):
    if x0 is None:
        starts, size = [(2 * i + z0) * 64 for i in range(4)], 64
    else:
        starts, size = [(2 * i + x0) * 16 for i in range(16)], 16
    rows = [xt_ref[pl.ds(pl.multiple_of(at, size), size), :] for at in starts]
    return jnp.concatenate(rows, axis=0)


def window_kernel(
    xt_ref, start_ref, own_ref, qe_ref, do_ref, w_ref, e_ref, dp_ref, lg_ref,
    ke_ref, ds_ref, dkv_ref, lat_mine_ref, lat_ref, theirs_a_ref, theirs_b_ref, xm_ref,
    total_ref,
):
    values = keys_and_values(xt_ref, w_ref, ke_ref)
    seen = iota((TOK, TOK), 0) - TOK >= start_ref[...]
    rope_grads = [jnp.zeros((TOK, 128), F32), jnp.zeros((TOK, 128), F32)]
    for h in range(HEADS):
        qe = qe_ref[h]
        do = do_ref[:, h * VDIM : (h + 1) * VDIM]
        scores = dot(ke_ref[h], qe, NT) * SCALING
        e = jnp.where(seen, jnp.exp(scores), 0.0)
        dp = dot(values[h], do, NT)
        norm = 1.0 / (lg_ref[h : h + 1, :] + jnp.sum(e, axis=0, keepdims=True))
        delta = (lg_ref[h + 4 : h + 5, :] + jnp.sum(e * dp, axis=0, keepdims=True)) * norm
        for half in range(2):
            if half == 1:
                e, dp = e_ref[h], dp_ref[h]
            probs = e * norm
            ds = (probs * (dp - delta) * SCALING).astype(BF16)
            ds_ref[h, half] = ds
            dk = dot(ds, qe)
            dkv_ref[half, :, h * PAIR : h * PAIR + NOPE] = dk[:, :NOPE].astype(BF16)
            rope_grads[half] = rope_grads[half] + dk[:, NOPE:]
            dkv_ref[half, :, h * PAIR + NOPE : (h + 1) * PAIR] = dot(
                probs.astype(BF16), do
            ).astype(BF16)
    z0, x0, core = (lax.axis_index(name) for name in ("z0", "x0", "core"))
    total_ref[:, :LATENT] = dot(dkv_ref[1], w_ref[...], NT)
    total_ref[:, LATENT : 2 * LATENT] = dot(dkv_ref[0], w_ref[...], NT)
    total_ref[:, 2 * LATENT :] = rope_grads[1] + pltpu.roll(rope_grads[0], ROPE, 1)
    for out_ref, parity in ((lat_mine_ref, core), (lat_ref, 1 - core)):
        for i in range(8):
            pair = [
                total_ref[pl.ds(pl.multiple_of((4 * i + 2 * j + parity) * 8, 8), 8), :]
                for j in range(2)
            ]
            out_ref[16 * i : 16 * i + 16, :] = jnp.concatenate(pair, axis=0).astype(out_ref.dtype)
    cut = HEADS * PAIR // 2
    sources = (xt_ref, own_ref)
    theirs_a_ref[...] = sum(
        dot(rows_of(sources[u], z0=1 - z0), dkv_ref[u, :, :cut]) for u in range(2)
    ).astype(BF16)
    theirs_b_ref[...] = sum(
        dot(rows_of(sources[u], x0=1 - x0), dkv_ref[u, :, cut:]) for u in range(2)
    ).astype(BF16)
    for u in range(2):
        xm_ref[0, u] = rows_of(sources[u], z0=z0)
        xm_ref[1, u] = rows_of(sources[u], x0=x0)


def core_sum_kernel(mine_ref, got_ref, out_ref):
    out_ref[...] = (mine_ref[...] + got_ref[...].astype(F32)).astype(BF16)


def query_kernel(kep_ref, keo_ref, ds_ref, dq_ref):
    for pair in range(HEADS // 2):
        parts = []
        for h in (2 * pair, 2 * pair + 1):
            parts.append(dot(ds_ref[h, 0], kep_ref[h], TN) + dot(ds_ref[h, 1], keo_ref[h], TN))
        moved = pltpu.roll(parts[1], ROPE, 1)
        base = pair * 2 * WIDTH
        dq_ref[:, base : base + 128] = parts[0][:, :128].astype(BF16)
        dq_ref[:, base + 128 : base + 256] = (parts[0][:, 128:] + moved[:, :128]).astype(BF16)
        dq_ref[:, base + 256 : base + 384] = moved[:, 128:].astype(BF16)


def first_sum_kernel(
    xm_ref, dkv_ref, got_a_ref, got_b_ref, kept_ref, send_a_ref, send_b_ref, a_ref, b_ref
):
    cut = HEADS * PAIR // 2
    a_ref[...] = got_a_ref[...].astype(F32) + sum(
        dot(xm_ref[0, u], dkv_ref[u, :, :cut]) for u in range(2)
    )
    b_ref[...] = got_b_ref[...].astype(F32) + sum(
        dot(xm_ref[1, u], dkv_ref[u, :, cut:]) for u in range(2)
    )
    z0, x0 = lax.axis_index("z0"), lax.axis_index("x0")
    for i in range(8):
        rows = slice(16 * i, 16 * i + 16)

        def of_a(x):
            return a_ref[pl.ds(pl.multiple_of((2 * i + x) * 16, 16), 16), :]

        def of_b(z):
            at = (i // 2) * 64 + z * 32 + (i % 2) * 16
            return b_ref[pl.ds(pl.multiple_of(at, 16), 16), :]

        kept_ref[rows, :cut] = of_a(x0)
        kept_ref[rows, cut:] = of_b(z0)
        send_a_ref[rows, :] = of_a(1 - x0).astype(BF16)
        send_b_ref[rows, :] = of_b(1 - z0).astype(BF16)


def second_sum_kernel(kept_ref, got_a_ref, got_b_ref, out_ref):
    cut = HEADS * PAIR // 2
    out_ref[:, :cut] = (kept_ref[:, :cut] + got_a_ref[...].astype(F32)).astype(BF16)
    out_ref[:, cut:] = (kept_ref[:, cut:] + got_b_ref[...].astype(F32)).astype(BF16)


def call(kernel, outs, flops, *args, scratch=()):
    return pl.pallas_call(
        kernel,
        out_shape=[jax.ShapeDtypeStruct(s, d) for s, d in outs],
        in_specs=[VMEM] * len(args),
        out_specs=[VMEM] * len(outs),
        scratch_shapes=list(scratch),
        compiler_params=pltpu.CompilerParams(vmem_limit_bytes=20 << 20),
        cost_estimate=pl.CostEstimate(flops=flops, bytes_accessed=4 << 20, transcendentals=0),
    )(*args)


def attend(own, prev, query, out_grad, up_weight, lengths):
    square = (HEADS, TOK, 256)
    columns = HEADS * PAIR
    keo, qe, e, dp, lg, start = call(
        own_kernel,
        [
            (square, BF16),
            (square, BF16),
            (square, F32),
            (square, F32),
            ((8, TOK), F32),
            ((1, TOK), jnp.int32),
        ],
        470_000_000, lengths.reshape(1, -1), own, query, out_grad, up_weight,
    )
    kep, ds, dkv, lat_mine, lat_theirs, theirs_a, theirs_b, xm = call(
        window_kernel,
        [
            (square, BF16),
            ((HEADS, 2, TOK, TOK), BF16),
            ((2, TOK, columns), BF16),
            ((TOK // 2, 2 * LATENT + 2 * ROPE), F32),
            ((TOK // 2, 2 * LATENT + 2 * ROPE), BF16),
            ((TOK, columns // 2), BF16),
            ((TOK, columns // 2), BF16),
            ((2, 2, TOK, TOK), BF16),
        ],
        1_700_000_000, prev, start, own, qe, out_grad, up_weight, e, dp, lg,
        scratch=[pltpu.VMEM((TOK, 2 * LATENT + 2 * ROPE), F32)],
    )
    return lat_mine, lat_theirs, theirs_a, theirs_b, (xm, dkv), (kep, keo, ds)


def query_grad(saved):
    return call(query_kernel, [((TOK, HEADS * WIDTH), BF16)], 270_000_000, *saved)[0]


def flip(x, mask):
    return lax.ppermute(x, CTX, [(i, i ^ mask) for i in range(32)])


def body(compressed, query, out_grad, up_weight, lengths):
    own = compressed.T
    prev = ctx_shift(own, 1)

    columns = HEADS * PAIR
    lat_mine, lat_theirs, theirs_a, theirs_b, factors, saved = attend(
        own, prev, query, out_grad, up_weight, lengths
    )
    got_core = lax.ppermute(lat_theirs, "core", [(0, 1), (1, 0)])
    got_a = flip(theirs_a, 4)
    got_b = flip(theirs_b, 1)
    (latent,) = call(core_sum_kernel, [(lat_mine.shape, BF16)], 1_000_000, lat_mine, got_core)
    parts = lax.all_to_all(latent.reshape(16, 8, -1), ("xh", "y"), 0, 0)
    kept, send_a, send_b = call(
        first_sum_kernel,
        [((128, columns), F32), ((128, columns // 2), BF16), ((128, columns // 2), BF16)],
        270_000_000, *factors, got_a, got_b,
        scratch=[pltpu.VMEM((TOK, columns // 2), F32)] * 2,
    )
    next_a = flip(send_a, 1)
    next_b = flip(send_b, 4)
    dq = query_grad(saved)
    (eighth,) = call(second_sum_kernel, [((128, columns), BF16)], 1_000_000, kept, next_a, next_b)
    eighths = lax.all_to_all(eighth.reshape(8, 16, -1), ("z2", "z1", "x1"), 0, 0)
    summed = jnp.sum(parts.astype(F32), axis=0)
    grad_weight = jnp.sum(eighths.astype(F32), axis=0)
    rope = 2 * LATENT + ROPE
    keep = jnp.concatenate([summed[:, :LATENT], summed[:, 2 * LATENT : rope]], axis=1)
    give = jnp.concatenate([summed[:, LATENT : 2 * LATENT], summed[:, rope:]], axis=1)
    grad_compressed = keep + ctx_shift(give, -1)
    return dq, grad_compressed, grad_weight


def solution(mesh):
    fine = Mesh(mesh.devices.reshape(2, 2, 2, 2, 2, 2, 8, 2), CTX + HEAD)
    placed = (P(CTX, None), P(CTX, HEAD), P(CTX, HEAD), P(None, HEAD), P())
    return jax.shard_map(
        body,
        mesh=fine,
        in_specs=placed,
        out_specs=(P(CTX, HEAD), P(CTX + HEAD, None), P(CTX, HEAD)),
        check_vma=False,
    )
```

```python
import math

import jax
import jax.numpy as jnp
from jax import lax
from jax.experimental import pallas as pl
from jax.experimental.pallas import tpu as pltpu
from jax.sharding import Mesh
from jax.sharding import PartitionSpec as P


LATENT = 512
ROPE = 64
NOPE = 128
VDIM = 128
HEADS = 4
TOK = 256
PAIR = NOPE + VDIM
WIDTH = NOPE + ROPE
SCALING = 1.0 / math.sqrt(WIDTH)
CTX = ("z2", "z1", "z0", "x1", "x0")
HEAD = ("xh", "y", "core")
F32 = jnp.float32
BF16 = jnp.bfloat16
NT = (((1,), (1,)), ((), ()))
TN = (((0,), (0,)), ((), ()))
VMEM = pl.BlockSpec(memory_space=pltpu.VMEM)


def dot(a, b, dims=(((1,), (0,)), ((), ()))):
    return lax.dot_general(a, b, dims, preferred_element_type=F32)


def ctx_shift(x, by):
    pairs = [(i, i + by) for i in range(32) if 0 <= i + by < 32]
    return lax.ppermute(x, CTX, pairs)


def iota(shape, dim):
    return lax.broadcasted_iota(jnp.int32, shape, dim)


def keys_and_values(xt_ref, w_ref, ke_ref):
    kv = dot(xt_ref[:LATENT, :], w_ref[...], TN).astype(BF16)
    rope = jnp.concatenate([xt_ref[LATENT:, :].astype(F32), jnp.zeros((ROPE, TOK), F32)], axis=0)
    rope = jnp.transpose(rope).astype(BF16)
    values = []
    for h in range(HEADS):
        ke_ref[h, :, :NOPE] = kv[:, h * PAIR : h * PAIR + NOPE]
        ke_ref[h, :, NOPE:] = rope
        values.append(kv[:, h * PAIR + NOPE : (h + 1) * PAIR])
    return values


def first_visible(len_ref):
    docs = len_ref.shape[1]
    lengths = jnp.broadcast_to(len_ref[...].astype(F32), (docs, docs))
    row, col = iota((docs, docs), 0), iota((docs, docs), 1)
    ends = jnp.sum(jnp.where(col <= row, lengths, 0.0), axis=1, keepdims=True)
    each = jnp.sum(jnp.where(col == row, lengths, 0.0), axis=1, keepdims=True)
    first = lax.axis_index(CTX) * TOK
    query = (iota((docs, TOK), 1) + first).astype(F32)
    before = jnp.sum(jnp.where(ends <= query, each, 0.0), axis=0, keepdims=True)
    return before.astype(jnp.int32) - first


def own_kernel(
    len_ref, xt_ref, q_ref, do_ref, w_ref, ke_ref, qe_ref, e_ref, dp_ref, lg_ref, start_ref
):
    start_ref[...] = first_visible(len_ref)
    lane = iota((TOK, 256), 1)
    for h in range(HEADS):
        base = (h // 2) * 2 * WIDTH
        if h % 2 == 0:
            rows = q_ref[:, base : base + 256].astype(F32)
        else:
            rows = pltpu.roll(q_ref[:, base + 128 : base + 384].astype(F32), 192, 1)
        qe_ref[h] = jnp.where(lane < WIDTH, rows, 0.0).astype(BF16)
    values = keys_and_values(xt_ref, w_ref, ke_ref)
    key = iota((TOK, TOK), 0)
    seen = (key >= start_ref[...]) & (key <= iota((TOK, TOK), 1))
    for h in range(HEADS):
        scores = dot(ke_ref[h], qe_ref[h], NT) * SCALING
        e = jnp.where(seen, jnp.exp(scores), 0.0)
        dp = dot(values[h], do_ref[:, h * VDIM : (h + 1) * VDIM], NT)
        e_ref[h] = e
        dp_ref[h] = dp
        lg_ref[h : h + 1, :] = jnp.sum(e, axis=0, keepdims=True)
        lg_ref[h + 4 : h + 5, :] = jnp.sum(e * dp, axis=0, keepdims=True)


def rows_of(xt_ref, z0=None, x0=None):
    if x0 is None:
        starts, size = [(2 * i + z0) * 64 for i in range(4)], 64
    else:
        starts, size = [(2 * i + x0) * 16 for i in range(16)], 16
    rows = [xt_ref[pl.ds(pl.multiple_of(at, size), size), :] for at in starts]
    return jnp.concatenate(rows, axis=0)


def window_kernel(
    xt_ref, start_ref, own_ref, qe_ref, do_ref, w_ref, e_ref, dp_ref, lg_ref,
    ke_ref, ds_ref, lat_mine_ref, lat_ref, theirs_a_ref, theirs_b_ref,
    mine_a_ref, mine_b_ref, total_ref, dkv_ref,
):
    values = keys_and_values(xt_ref, w_ref, ke_ref)
    seen = iota((TOK, TOK), 0) - TOK >= start_ref[...]
    rope_grads = [jnp.zeros((TOK, 128), F32), jnp.zeros((TOK, 128), F32)]
    for h in range(HEADS):
        qe = qe_ref[h]
        do = do_ref[:, h * VDIM : (h + 1) * VDIM]
        scores = dot(ke_ref[h], qe, NT) * SCALING
        e = jnp.where(seen, jnp.exp(scores), 0.0)
        dp = dot(values[h], do, NT)
        norm = 1.0 / (lg_ref[h : h + 1, :] + jnp.sum(e, axis=0, keepdims=True))
        delta = (lg_ref[h + 4 : h + 5, :] + jnp.sum(e * dp, axis=0, keepdims=True)) * norm
        for half in range(2):
            if half == 1:
                e, dp = e_ref[h], dp_ref[h]
            probs = e * norm
            ds = (probs * (dp - delta) * SCALING).astype(BF16)
            ds_ref[h, half] = ds
            dk = dot(ds, qe)
            dkv_ref[half, :, h * PAIR : h * PAIR + NOPE] = dk[:, :NOPE].astype(BF16)
            rope_grads[half] = rope_grads[half] + dk[:, NOPE:]
            dkv_ref[half, :, h * PAIR + NOPE : (h + 1) * PAIR] = dot(
                probs.astype(BF16), do
            ).astype(BF16)
    z0, x0, core = (lax.axis_index(name) for name in ("z0", "x0", "core"))
    total_ref[:, :LATENT] = dot(dkv_ref[1], w_ref[...], NT)
    total_ref[:, LATENT : 2 * LATENT] = dot(dkv_ref[0], w_ref[...], NT)
    total_ref[:, 2 * LATENT :] = rope_grads[1] + pltpu.roll(rope_grads[0], ROPE, 1)
    for out_ref, parity in ((lat_mine_ref, core), (lat_ref, 1 - core)):
        for i in range(8):
            pair = [
                total_ref[pl.ds(pl.multiple_of((16 * j + 2 * i + parity) * 8, 8), 8), :]
                for j in range(2)
            ]
            out_ref[16 * i : 16 * i + 16, :] = jnp.concatenate(pair, axis=0).astype(out_ref.dtype)
    cut = HEADS * PAIR // 2
    sources = (xt_ref, own_ref)
    theirs_a_ref[...] = sum(
        dot(rows_of(sources[u], z0=1 - z0), dkv_ref[u, :, :cut]) for u in range(2)
    ).astype(BF16)
    theirs_b_ref[...] = sum(
        dot(rows_of(sources[u], x0=1 - x0), dkv_ref[u, :, cut:]) for u in range(2)
    ).astype(BF16)
    mine_a_ref[...] = sum(dot(rows_of(sources[u], z0=z0), dkv_ref[u, :, :cut]) for u in range(2))
    mine_b_ref[...] = sum(dot(rows_of(sources[u], x0=x0), dkv_ref[u, :, cut:]) for u in range(2))


def core_sum_kernel(mine_ref, got_ref, out_ref):
    out_ref[...] = (mine_ref[...] + got_ref[...].astype(F32)).astype(BF16)


def query_kernel(kep_ref, keo_ref, ds_ref, dq_ref):
    for pair in range(HEADS // 2):
        parts = []
        for h in (2 * pair, 2 * pair + 1):
            parts.append(dot(ds_ref[h, 0], kep_ref[h], TN) + dot(ds_ref[h, 1], keo_ref[h], TN))
        moved = pltpu.roll(parts[1], ROPE, 1)
        base = pair * 2 * WIDTH
        dq_ref[:, base : base + 128] = parts[0][:, :128].astype(BF16)
        dq_ref[:, base + 128 : base + 256] = (parts[0][:, 128:] + moved[:, :128]).astype(BF16)
        dq_ref[:, base + 256 : base + 384] = moved[:, 128:].astype(BF16)


def first_sum_kernel(
    mine_a_ref, mine_b_ref, got_a_ref, got_b_ref, kept_ref, send_a_ref, send_b_ref, a_ref, b_ref
):
    cut = HEADS * PAIR // 2
    a_ref[...] = mine_a_ref[...] + got_a_ref[...].astype(F32)
    b_ref[...] = mine_b_ref[...] + got_b_ref[...].astype(F32)
    z0, x0 = lax.axis_index("z0"), lax.axis_index("x0")
    for i in range(8):
        rows = slice(16 * i, 16 * i + 16)

        def of_a(x):
            return a_ref[pl.ds(pl.multiple_of((2 * i + x) * 16, 16), 16), :]

        def of_b(z):
            at = (i // 2) * 64 + z * 32 + (i % 2) * 16
            return b_ref[pl.ds(pl.multiple_of(at, 16), 16), :]

        kept_ref[rows, :cut] = of_a(x0)
        kept_ref[rows, cut:] = of_b(z0)
        send_a_ref[rows, :] = of_a(1 - x0).astype(BF16)
        send_b_ref[rows, :] = of_b(1 - z0).astype(BF16)


def second_sum_kernel(kept_ref, got_a_ref, got_b_ref, out_ref):
    cut = HEADS * PAIR // 2
    out_ref[:, :cut] = (kept_ref[:, :cut] + got_a_ref[...].astype(F32)).astype(BF16)
    out_ref[:, cut:] = (kept_ref[:, cut:] + got_b_ref[...].astype(F32)).astype(BF16)


def head_sum_kernel(parts_ref, mine_ref, send_ref, sum_ref):
    total = parts_ref[0].astype(F32)
    for i in range(1, 8):
        total = total + parts_ref[i].astype(F32)
    sum_ref[...] = total
    xh = lax.axis_index("xh")
    mine_ref[...] = sum_ref[pl.ds(pl.multiple_of(xh * 8, 8), 8), :]
    send_ref[...] = sum_ref[pl.ds(pl.multiple_of((1 - xh) * 8, 8), 8), :].astype(BF16)


def part_kernel(mine_ref, got_ref, keep_ref, give_ref):
    total = mine_ref[...] + got_ref[...].astype(F32)
    keep_ref[:, :LATENT] = total[:, :LATENT]
    give_ref[:, :LATENT] = total[:, LATENT : 2 * LATENT]
    rope = total[:, 2 * LATENT :]
    keep_ref[:, LATENT:] = rope[:, :ROPE]
    give_ref[:, LATENT:] = pltpu.roll(rope, ROPE, 1)[:, :ROPE]


def call(kernel, outs, flops, *args, scratch=()):
    return pl.pallas_call(
        kernel,
        out_shape=[jax.ShapeDtypeStruct(s, d) for s, d in outs],
        in_specs=[VMEM] * len(args),
        out_specs=[VMEM] * len(outs),
        scratch_shapes=list(scratch),
        compiler_params=pltpu.CompilerParams(vmem_limit_bytes=20 << 20),
        cost_estimate=pl.CostEstimate(flops=flops, bytes_accessed=4 << 20, transcendentals=0),
    )(*args)


def attend(own, prev, query, out_grad, up_weight, lengths):
    square = (HEADS, TOK, 256)
    columns = HEADS * PAIR
    keo, qe, e, dp, lg, start = call(
        own_kernel,
        [
            (square, BF16),
            (square, BF16),
            (square, F32),
            (square, F32),
            ((8, TOK), F32),
            ((1, TOK), jnp.int32),
        ],
        470_000_000, lengths.reshape(1, -1), own, query, out_grad, up_weight,
    )
    kep, ds, lat_mine, lat_theirs, theirs_a, theirs_b, *mine = call(
        window_kernel,
        [
            (square, BF16),
            ((HEADS, 2, TOK, TOK), BF16),
            ((TOK // 2, 2 * LATENT + 2 * ROPE), F32),
            ((TOK // 2, 2 * LATENT + 2 * ROPE), BF16),
            ((TOK, columns // 2), BF16),
            ((TOK, columns // 2), BF16),
            ((TOK, columns // 2), F32),
            ((TOK, columns // 2), F32),
        ],
        1_700_000_000, prev, start, own, qe, out_grad, up_weight, e, dp, lg,
        scratch=[
            pltpu.VMEM((TOK, 2 * LATENT + 2 * ROPE), F32),
            pltpu.VMEM((2, TOK, columns), BF16),
        ],
    )
    return lat_mine, lat_theirs, theirs_a, theirs_b, mine, (kep, keo, ds)


def query_grad(saved):
    return call(query_kernel, [((TOK, HEADS * WIDTH), BF16)], 270_000_000, *saved)[0]


def flip(x, mask):
    return lax.ppermute(x, CTX, [(i, i ^ mask) for i in range(32)])


def body(compressed, query, out_grad, up_weight, lengths):
    own = compressed.T
    prev = ctx_shift(own, 1)

    columns = HEADS * PAIR
    lat_mine, lat_theirs, theirs_a, theirs_b, mine, saved = attend(
        own, prev, query, out_grad, up_weight, lengths
    )
    got_core = lax.ppermute(lat_theirs, "core", [(0, 1), (1, 0)])
    got_a = flip(theirs_a, 4)
    got_b = flip(theirs_b, 1)
    (latent,) = call(core_sum_kernel, [(lat_mine.shape, BF16)], 1_000_000, lat_mine, got_core)
    parts = lax.all_to_all(latent.reshape(8, 16, -1), "y", 0, 0)
    kept, send_a, send_b = call(
        first_sum_kernel,
        [((128, columns), F32), ((128, columns // 2), BF16), ((128, columns // 2), BF16)],
        1_000_000, *mine, got_a, got_b,
        scratch=[pltpu.VMEM((TOK, columns // 2), F32)] * 2,
    )
    next_a = flip(send_a, 1)
    next_b = flip(send_b, 4)
    dq = query_grad(saved)
    (eighth,) = call(second_sum_kernel, [((128, columns), BF16)], 1_000_000, kept, next_a, next_b)
    eighths = lax.all_to_all(eighth.reshape(8, 16, -1), ("z2", "z1", "x1"), 0, 0)
    rows = (8, 2 * LATENT + 2 * ROPE)
    kept_rows, sent_rows = call(
        head_sum_kernel,
        [(rows, F32), (rows, BF16)],
        1_000_000, parts,
        scratch=[pltpu.VMEM((16, rows[1]), F32)],
    )
    pairs = [(0, 1), (1, 0)]
    got_rows = lax.ppermute(sent_rows, "xh", pairs)
    keep, give = call(part_kernel, [((8, LATENT + ROPE), F32)] * 2, 1_000_000, kept_rows, got_rows)
    grad_compressed = keep + ctx_shift(give, -1)
    grad_weight = jnp.sum(eighths.astype(F32), axis=0)
    return dq, grad_compressed, grad_weight


def solution(mesh):
    fine = Mesh(mesh.devices.reshape(2, 2, 2, 2, 2, 2, 8, 2), CTX + HEAD)
    placed = (P(CTX, None), P(CTX, HEAD), P(CTX, HEAD), P(None, HEAD), P())
    return jax.shard_map(
        body,
        mesh=fine,
        in_specs=placed,
        out_specs=(P(CTX, HEAD), P(CTX + HEAD, None), P(CTX, HEAD)),
        check_vma=False,
    )
```

```python
import math

import jax
import jax.numpy as jnp
from jax import lax
from jax.experimental import pallas as pl
from jax.experimental.pallas import tpu as pltpu
from jax.sharding import Mesh
from jax.sharding import PartitionSpec as P


LATENT = 512
ROPE = 64
NOPE = 128
VDIM = 128
HEADS = 4
TOK = 256
PAIR = NOPE + VDIM
WIDTH = NOPE + ROPE
SCALING = 1.0 / math.sqrt(WIDTH)
CTX = ("z2", "z1", "z0", "x1", "x0")
HEAD = ("xh", "y", "core")
F32 = jnp.float32
BF16 = jnp.bfloat16
NT = (((1,), (1,)), ((), ()))
TN = (((0,), (0,)), ((), ()))
VMEM = pl.BlockSpec(memory_space=pltpu.VMEM)


def dot(a, b, dims=(((1,), (0,)), ((), ()))):
    return lax.dot_general(a, b, dims, preferred_element_type=F32)


def ctx_shift(x, by):
    pairs = [(i, i + by) for i in range(32) if 0 <= i + by < 32]
    return lax.ppermute(x, CTX, pairs)


def iota(shape, dim):
    return lax.broadcasted_iota(jnp.int32, shape, dim)


def keys_and_values(xt_ref, w_ref, ke_ref):
    kv = dot(xt_ref[:LATENT, :], w_ref[...], TN).astype(BF16)
    rope = jnp.concatenate([xt_ref[LATENT:, :].astype(F32), jnp.zeros((ROPE, TOK), F32)], axis=0)
    rope = jnp.transpose(rope).astype(BF16)
    values = []
    for h in range(HEADS):
        ke_ref[h, :, :NOPE] = kv[:, h * PAIR : h * PAIR + NOPE]
        ke_ref[h, :, NOPE:] = rope
        values.append(kv[:, h * PAIR + NOPE : (h + 1) * PAIR])
    return values


def first_visible(len_ref):
    docs = len_ref.shape[1]
    lengths = jnp.broadcast_to(len_ref[...].astype(F32), (docs, docs))
    row, col = iota((docs, docs), 0), iota((docs, docs), 1)
    ends = jnp.sum(jnp.where(col <= row, lengths, 0.0), axis=1, keepdims=True)
    each = jnp.sum(jnp.where(col == row, lengths, 0.0), axis=1, keepdims=True)
    first = lax.axis_index(CTX) * TOK
    query = (iota((docs, TOK), 1) + first).astype(F32)
    before = jnp.sum(jnp.where(ends <= query, each, 0.0), axis=0, keepdims=True)
    return before.astype(jnp.int32) - first


def own_kernel(
    len_ref, xt_ref, q_ref, do_ref, w_ref, ke_ref, qe_ref, e_ref, dp_ref, lg_ref, start_ref
):
    start_ref[...] = first_visible(len_ref)
    lane = iota((TOK, 256), 1)
    for h in range(HEADS):
        base = (h // 2) * 2 * WIDTH
        if h % 2 == 0:
            rows = q_ref[:, base : base + 256].astype(F32)
        else:
            rows = pltpu.roll(q_ref[:, base + 128 : base + 384].astype(F32), 192, 1)
        qe_ref[h] = jnp.where(lane < WIDTH, rows, 0.0).astype(BF16)
    values = keys_and_values(xt_ref, w_ref, ke_ref)
    key = iota((TOK, TOK), 0)
    seen = (key >= start_ref[...]) & (key <= iota((TOK, TOK), 1))
    for h in range(HEADS):
        scores = dot(ke_ref[h], qe_ref[h], NT) * SCALING
        e = jnp.where(seen, jnp.exp(scores), 0.0)
        dp = dot(values[h], do_ref[:, h * VDIM : (h + 1) * VDIM], NT)
        e_ref[h] = e
        dp_ref[h] = dp
        lg_ref[h : h + 1, :] = jnp.sum(e, axis=0, keepdims=True)
        lg_ref[h + 4 : h + 5, :] = jnp.sum(e * dp, axis=0, keepdims=True)


def rows_of(xt_ref, z0):
    rows = [xt_ref[pl.ds(pl.multiple_of((2 * i + z0) * 64, 64), 64), :] for i in range(4)]
    return jnp.concatenate(rows, axis=0)


def window_kernel(
    xt_ref, start_ref, own_ref, qe_ref, do_ref, w_ref, e_ref, dp_ref, lg_ref,
    ke_ref, ds_ref, lat_mine_ref, lat_ref, theirs_ref, mine_ref, total_ref, dkv_ref,
):
    values = keys_and_values(xt_ref, w_ref, ke_ref)
    seen = iota((TOK, TOK), 0) - TOK >= start_ref[...]
    rope_grads = [jnp.zeros((TOK, 128), F32), jnp.zeros((TOK, 128), F32)]
    for h in range(HEADS):
        qe = qe_ref[h]
        do = do_ref[:, h * VDIM : (h + 1) * VDIM]
        scores = dot(ke_ref[h], qe, NT) * SCALING
        e = jnp.where(seen, jnp.exp(scores), 0.0)
        dp = dot(values[h], do, NT)
        norm = 1.0 / (lg_ref[h : h + 1, :] + jnp.sum(e, axis=0, keepdims=True))
        delta = (lg_ref[h + 4 : h + 5, :] + jnp.sum(e * dp, axis=0, keepdims=True)) * norm
        for half in range(2):
            if half == 1:
                e, dp = e_ref[h], dp_ref[h]
            probs = e * norm
            ds = (probs * (dp - delta) * SCALING).astype(BF16)
            ds_ref[h, half] = ds
            dk = dot(ds, qe)
            dkv_ref[half, :, h * PAIR : h * PAIR + NOPE] = dk[:, :NOPE].astype(BF16)
            rope_grads[half] = rope_grads[half] + dk[:, NOPE:]
            dkv_ref[half, :, h * PAIR + NOPE : (h + 1) * PAIR] = dot(
                probs.astype(BF16), do
            ).astype(BF16)
    z0, core = lax.axis_index("z0"), lax.axis_index("core")
    total_ref[:, :LATENT] = dot(dkv_ref[1], w_ref[...], NT)
    total_ref[:, LATENT : 2 * LATENT] = dot(dkv_ref[0], w_ref[...], NT)
    total_ref[:, 2 * LATENT :] = rope_grads[1] + pltpu.roll(rope_grads[0], ROPE, 1)
    for out_ref, parity in ((lat_mine_ref, core), (lat_ref, 1 - core)):
        for i in range(8):
            pair = [
                total_ref[pl.ds(pl.multiple_of((4 * i + 2 * j + parity) * 8, 8), 8), :]
                for j in range(2)
            ]
            out_ref[16 * i : 16 * i + 16, :] = jnp.concatenate(pair, axis=0).astype(out_ref.dtype)
    sources = (xt_ref, own_ref)
    theirs_ref[...] = sum(dot(rows_of(sources[u], 1 - z0), dkv_ref[u]) for u in range(2)).astype(BF16)
    mine_ref[...] = sum(dot(rows_of(sources[u], z0), dkv_ref[u]) for u in range(2))


def pair_sum_kernel(mine_ref, got_ref, out_ref):
    out_ref[...] = (mine_ref[...] + got_ref[...].astype(F32)).astype(BF16)


def query_kernel(kep_ref, keo_ref, ds_ref, dq_ref):
    for pair in range(HEADS // 2):
        parts = []
        for h in (2 * pair, 2 * pair + 1):
            parts.append(dot(ds_ref[h, 0], kep_ref[h], TN) + dot(ds_ref[h, 1], keo_ref[h], TN))
        moved = pltpu.roll(parts[1], ROPE, 1)
        base = pair * 2 * WIDTH
        dq_ref[:, base : base + 128] = parts[0][:, :128].astype(BF16)
        dq_ref[:, base + 128 : base + 256] = (parts[0][:, 128:] + moved[:, :128]).astype(BF16)
        dq_ref[:, base + 256 : base + 384] = moved[:, 128:].astype(BF16)


def first_sum_kernel(mine_ref, got_ref, kept_ref, send_ref, sum_ref):
    sum_ref[...] = mine_ref[...] + got_ref[...].astype(F32)
    x0 = lax.axis_index("x0")
    for i in range(8):
        rows = slice(16 * i, 16 * i + 16)
        kept_ref[rows, :] = sum_ref[pl.ds(pl.multiple_of((2 * i + x0) * 16, 16), 16), :]
        send_ref[rows, :] = sum_ref[
            pl.ds(pl.multiple_of((2 * i + 1 - x0) * 16, 16), 16), :
        ].astype(BF16)


def head_sum_kernel(parts_ref, keep_ref, give_ref):
    total = parts_ref[0].astype(F32)
    for i in range(1, 16):
        total = total + parts_ref[i].astype(F32)
    keep_ref[:, :LATENT] = total[:, :LATENT]
    give_ref[:, :LATENT] = total[:, LATENT : 2 * LATENT]
    rope = total[:, 2 * LATENT :]
    keep_ref[:, LATENT:] = rope[:, :ROPE]
    give_ref[:, LATENT:] = pltpu.roll(rope, ROPE, 1)[:, :ROPE]


def call(kernel, outs, flops, *args, scratch=()):
    return pl.pallas_call(
        kernel,
        out_shape=[jax.ShapeDtypeStruct(s, d) for s, d in outs],
        in_specs=[VMEM] * len(args),
        out_specs=[VMEM] * len(outs),
        scratch_shapes=list(scratch),
        compiler_params=pltpu.CompilerParams(vmem_limit_bytes=20 << 20),
        cost_estimate=pl.CostEstimate(flops=flops, bytes_accessed=4 << 20, transcendentals=0),
    )(*args)


def attend(own, prev, query, out_grad, up_weight, lengths):
    square = (HEADS, TOK, 256)
    columns = HEADS * PAIR
    keo, qe, e, dp, lg, start = call(
        own_kernel,
        [
            (square, BF16),
            (square, BF16),
            (square, F32),
            (square, F32),
            ((8, TOK), F32),
            ((1, TOK), jnp.int32),
        ],
        470_000_000, lengths.reshape(1, -1), own, query, out_grad, up_weight,
    )
    kep, ds, lat_mine, lat_theirs, theirs, mine = call(
        window_kernel,
        [
            (square, BF16),
            ((HEADS, 2, TOK, TOK), BF16),
            ((TOK // 2, 2 * LATENT + 2 * ROPE), F32),
            ((TOK // 2, 2 * LATENT + 2 * ROPE), BF16),
            ((TOK, columns), BF16),
            ((TOK, columns), F32),
        ],
        1_700_000_000, prev, start, own, qe, out_grad, up_weight, e, dp, lg,
        scratch=[
            pltpu.VMEM((TOK, 2 * LATENT + 2 * ROPE), F32),
            pltpu.VMEM((2, TOK, columns), BF16),
        ],
    )
    return lat_mine, lat_theirs, theirs, mine, (kep, keo, ds)


def query_grad(saved):
    return call(query_kernel, [((TOK, HEADS * WIDTH), BF16)], 270_000_000, *saved)[0]


def flip(x, mask):
    return lax.ppermute(x, CTX, [(i, i ^ mask) for i in range(32)])


def body(compressed, query, out_grad, up_weight, lengths):
    own = compressed.T
    prev = ctx_shift(own, 1)

    columns = HEADS * PAIR
    lat_mine, lat_theirs, theirs, mine, saved = attend(
        own, prev, query, out_grad, up_weight, lengths
    )
    got_core = lax.ppermute(lat_theirs, "core", [(0, 1), (1, 0)])
    got_z = flip(theirs, 4)
    (latent,) = call(pair_sum_kernel, [(lat_mine.shape, BF16)], 1_000_000, lat_mine, got_core)
    parts = lax.all_to_all(latent.reshape(16, 8, -1), ("xh", "y"), 0, 0)
    kept, send = call(
        first_sum_kernel,
        [((128, columns), F32), ((128, columns), BF16)],
        1_000_000, mine, got_z,
        scratch=[pltpu.VMEM((TOK, columns), F32)],
    )
    got_x = flip(send, 1)
    dq = query_grad(saved)
    (eighth,) = call(pair_sum_kernel, [((128, columns), BF16)], 1_000_000, kept, got_x)
    eighths = lax.all_to_all(eighth.reshape(8, 16, -1), ("z2", "z1", "x1"), 0, 0)
    keep, give = call(head_sum_kernel, [((8, LATENT + ROPE), F32)] * 2, 1_000_000, parts)
    grad_compressed = keep + ctx_shift(give, -1)
    grad_weight = jnp.sum(eighths.astype(F32), axis=0)
    return dq, grad_compressed, grad_weight


def solution(mesh):
    fine = Mesh(mesh.devices.reshape(2, 2, 2, 2, 2, 2, 8, 2), CTX + HEAD)
    placed = (P(CTX, None), P(CTX, HEAD), P(CTX, HEAD), P(None, HEAD), P())
    return jax.shard_map(
        body,
        mesh=fine,
        in_specs=placed,
        out_specs=(P(CTX, HEAD), P(CTX + HEAD, None), P(CTX, HEAD)),
        check_vma=False,
    )
```

```python
import math

import jax
import jax.numpy as jnp
from jax import lax
from jax.experimental import pallas as pl
from jax.experimental.pallas import tpu as pltpu
from jax.sharding import Mesh
from jax.sharding import PartitionSpec as P


LATENT = 512
ROPE = 64
NOPE = 128
VDIM = 128
HEADS = 4
TOK = 256
PAIR = NOPE + VDIM
WIDTH = NOPE + ROPE
SCALING = 1.0 / math.sqrt(WIDTH)
CTX = ("z2", "z1", "z0", "x1", "x0")
HEAD = ("xh", "y", "core")
F32 = jnp.float32
BF16 = jnp.bfloat16
NT = (((1,), (1,)), ((), ()))
TN = (((0,), (0,)), ((), ()))
VMEM = pl.BlockSpec(memory_space=pltpu.VMEM)


def dot(a, b, dims=(((1,), (0,)), ((), ()))):
    return lax.dot_general(a, b, dims, preferred_element_type=F32)


def ctx_shift(x, by):
    pairs = [(i, i + by) for i in range(32) if 0 <= i + by < 32]
    return lax.ppermute(x, CTX, pairs)


def iota(shape, dim):
    return lax.broadcasted_iota(jnp.int32, shape, dim)


def keys_and_values(xt_ref, w_ref, ke_ref):
    kv = dot(xt_ref[:LATENT, :], w_ref[...], TN).astype(BF16)
    rope = jnp.concatenate([xt_ref[LATENT:, :].astype(F32), jnp.zeros((ROPE, TOK), F32)], axis=0)
    rope = jnp.transpose(rope).astype(BF16)
    values = []
    for h in range(HEADS):
        ke_ref[h, :, :NOPE] = kv[:, h * PAIR : h * PAIR + NOPE]
        ke_ref[h, :, NOPE:] = rope
        values.append(kv[:, h * PAIR + NOPE : (h + 1) * PAIR])
    return values


def first_visible(len_ref):
    docs = len_ref.shape[1]
    lengths = jnp.broadcast_to(len_ref[...].astype(F32), (docs, docs))
    row, col = iota((docs, docs), 0), iota((docs, docs), 1)
    ends = jnp.sum(jnp.where(col <= row, lengths, 0.0), axis=1, keepdims=True)
    each = jnp.sum(jnp.where(col == row, lengths, 0.0), axis=1, keepdims=True)
    first = lax.axis_index(CTX) * TOK
    query = (iota((docs, TOK), 1) + first).astype(F32)
    before = jnp.sum(jnp.where(ends <= query, each, 0.0), axis=0, keepdims=True)
    return before.astype(jnp.int32) - first


def own_kernel(
    len_ref, xt_ref, q_ref, do_ref, w_ref, ke_ref, qe_ref, e_ref, dp_ref, lg_ref, start_ref
):
    start_ref[...] = first_visible(len_ref)
    lane = iota((TOK, 256), 1)
    for h in range(HEADS):
        base = (h // 2) * 2 * WIDTH
        if h % 2 == 0:
            rows = q_ref[:, base : base + 256].astype(F32)
        else:
            rows = pltpu.roll(q_ref[:, base + 128 : base + 384].astype(F32), 192, 1)
        qe_ref[h] = jnp.where(lane < WIDTH, rows, 0.0).astype(BF16)
    values = keys_and_values(xt_ref, w_ref, ke_ref)
    key = iota((TOK, TOK), 0)
    seen = (key >= start_ref[...]) & (key <= iota((TOK, TOK), 1))
    for h in range(HEADS):
        scores = dot(ke_ref[h], qe_ref[h], NT) * SCALING
        e = jnp.where(seen, jnp.exp(scores), 0.0)
        dp = dot(values[h], do_ref[:, h * VDIM : (h + 1) * VDIM], NT)
        e_ref[h] = e
        dp_ref[h] = dp
        lg_ref[h : h + 1, :] = jnp.sum(e, axis=0, keepdims=True)
        lg_ref[h + 4 : h + 5, :] = jnp.sum(e * dp, axis=0, keepdims=True)


def rows_of(xt_ref, x0):
    rows = [xt_ref[pl.ds(pl.multiple_of((2 * i + x0) * 16, 16), 16), :] for i in range(16)]
    return jnp.concatenate(rows, axis=0)


def window_kernel(
    xt_ref, start_ref, own_ref, qe_ref, do_ref, w_ref, e_ref, dp_ref, lg_ref,
    ke_ref, ds_ref, lat_mine_ref, lat_ref, theirs_ref, mine_ref, total_ref, dkv_ref,
):
    values = keys_and_values(xt_ref, w_ref, ke_ref)
    seen = iota((TOK, TOK), 0) - TOK >= start_ref[...]
    rope_grads = [jnp.zeros((TOK, 128), F32), jnp.zeros((TOK, 128), F32)]
    for h in range(HEADS):
        qe = qe_ref[h]
        do = do_ref[:, h * VDIM : (h + 1) * VDIM]
        scores = dot(ke_ref[h], qe, NT) * SCALING
        e = jnp.where(seen, jnp.exp(scores), 0.0)
        dp = dot(values[h], do, NT)
        norm = 1.0 / (lg_ref[h : h + 1, :] + jnp.sum(e, axis=0, keepdims=True))
        delta = (lg_ref[h + 4 : h + 5, :] + jnp.sum(e * dp, axis=0, keepdims=True)) * norm
        for half in range(2):
            if half == 1:
                e, dp = e_ref[h], dp_ref[h]
            probs = e * norm
            ds = (probs * (dp - delta) * SCALING).astype(BF16)
            ds_ref[h, half] = ds
            dk = dot(ds, qe)
            dkv_ref[half, :, h * PAIR : h * PAIR + NOPE] = dk[:, :NOPE].astype(BF16)
            rope_grads[half] = rope_grads[half] + dk[:, NOPE:]
            dkv_ref[half, :, h * PAIR + NOPE : (h + 1) * PAIR] = dot(
                probs.astype(BF16), do
            ).astype(BF16)
    x0, core = lax.axis_index("x0"), lax.axis_index("core")
    total_ref[:, :LATENT] = dot(dkv_ref[1], w_ref[...], NT)
    total_ref[:, LATENT : 2 * LATENT] = dot(dkv_ref[0], w_ref[...], NT)
    total_ref[:, 2 * LATENT :] = rope_grads[1] + pltpu.roll(rope_grads[0], ROPE, 1)
    for out_ref, parity in ((lat_mine_ref, core), (lat_ref, 1 - core)):
        for i in range(8):
            pair = [
                total_ref[pl.ds(pl.multiple_of((4 * i + 2 * j + parity) * 8, 8), 8), :]
                for j in range(2)
            ]
            out_ref[16 * i : 16 * i + 16, :] = jnp.concatenate(pair, axis=0).astype(out_ref.dtype)
    sources = (xt_ref, own_ref)
    theirs_ref[...] = sum(dot(rows_of(sources[u], 1 - x0), dkv_ref[u]) for u in range(2)).astype(BF16)
    mine_ref[...] = sum(dot(rows_of(sources[u], x0), dkv_ref[u]) for u in range(2))


def pair_sum_kernel(mine_ref, got_ref, out_ref):
    out_ref[...] = (mine_ref[...] + got_ref[...].astype(F32)).astype(BF16)


def query_kernel(kep_ref, keo_ref, ds_ref, dq_ref):
    for pair in range(HEADS // 2):
        parts = []
        for h in (2 * pair, 2 * pair + 1):
            parts.append(dot(ds_ref[h, 0], kep_ref[h], TN) + dot(ds_ref[h, 1], keo_ref[h], TN))
        moved = pltpu.roll(parts[1], ROPE, 1)
        base = pair * 2 * WIDTH
        dq_ref[:, base : base + 128] = parts[0][:, :128].astype(BF16)
        dq_ref[:, base + 128 : base + 256] = (parts[0][:, 128:] + moved[:, :128]).astype(BF16)
        dq_ref[:, base + 256 : base + 384] = moved[:, 128:].astype(BF16)


def first_sum_kernel(mine_ref, got_ref, kept_ref, send_ref, sum_ref):
    sum_ref[...] = mine_ref[...] + got_ref[...].astype(F32)
    z0 = lax.axis_index("z0")
    for i in range(8):
        rows = slice(16 * i, 16 * i + 16)
        base = (i // 2) * 64 + (i % 2) * 16
        kept_ref[rows, :] = sum_ref[pl.ds(pl.multiple_of(base + z0 * 32, 16), 16), :]
        send_ref[rows, :] = sum_ref[
            pl.ds(pl.multiple_of(base + (1 - z0) * 32, 16), 16), :
        ].astype(BF16)


def head_sum_kernel(parts_ref, keep_ref, give_ref):
    total = parts_ref[0].astype(F32)
    for i in range(1, 16):
        total = total + parts_ref[i].astype(F32)
    keep_ref[:, :LATENT] = total[:, :LATENT]
    give_ref[:, :LATENT] = total[:, LATENT : 2 * LATENT]
    rope = total[:, 2 * LATENT :]
    keep_ref[:, LATENT:] = rope[:, :ROPE]
    give_ref[:, LATENT:] = pltpu.roll(rope, ROPE, 1)[:, :ROPE]


def call(kernel, outs, flops, *args, scratch=()):
    return pl.pallas_call(
        kernel,
        out_shape=[jax.ShapeDtypeStruct(s, d) for s, d in outs],
        in_specs=[VMEM] * len(args),
        out_specs=[VMEM] * len(outs),
        scratch_shapes=list(scratch),
        compiler_params=pltpu.CompilerParams(vmem_limit_bytes=20 << 20),
        cost_estimate=pl.CostEstimate(flops=flops, bytes_accessed=4 << 20, transcendentals=0),
    )(*args)


def attend(own, prev, query, out_grad, up_weight, lengths):
    square = (HEADS, TOK, 256)
    columns = HEADS * PAIR
    keo, qe, e, dp, lg, start = call(
        own_kernel,
        [
            (square, BF16),
            (square, BF16),
            (square, F32),
            (square, F32),
            ((8, TOK), F32),
            ((1, TOK), jnp.int32),
        ],
        470_000_000, lengths.reshape(1, -1), own, query, out_grad, up_weight,
    )
    kep, ds, lat_mine, lat_theirs, theirs, mine = call(
        window_kernel,
        [
            (square, BF16),
            ((HEADS, 2, TOK, TOK), BF16),
            ((TOK // 2, 2 * LATENT + 2 * ROPE), F32),
            ((TOK // 2, 2 * LATENT + 2 * ROPE), BF16),
            ((TOK, columns), BF16),
            ((TOK, columns), F32),
        ],
        1_700_000_000, prev, start, own, qe, out_grad, up_weight, e, dp, lg,
        scratch=[
            pltpu.VMEM((TOK, 2 * LATENT + 2 * ROPE), F32),
            pltpu.VMEM((2, TOK, columns), BF16),
        ],
    )
    return lat_mine, lat_theirs, theirs, mine, (kep, keo, ds)


def query_grad(saved):
    return call(query_kernel, [((TOK, HEADS * WIDTH), BF16)], 270_000_000, *saved)[0]


def flip(x, mask):
    return lax.ppermute(x, CTX, [(i, i ^ mask) for i in range(32)])


def body(compressed, query, out_grad, up_weight, lengths):
    own = compressed.T
    prev = ctx_shift(own, 1)

    columns = HEADS * PAIR
    lat_mine, lat_theirs, theirs, mine, saved = attend(
        own, prev, query, out_grad, up_weight, lengths
    )
    got_core = lax.ppermute(lat_theirs, "core", [(0, 1), (1, 0)])
    got_x = flip(theirs, 1)
    (latent,) = call(pair_sum_kernel, [(lat_mine.shape, BF16)], 1_000_000, lat_mine, got_core)
    parts = lax.all_to_all(latent.reshape(16, 8, -1), ("xh", "y"), 0, 0)
    kept, send = call(
        first_sum_kernel,
        [((128, columns), F32), ((128, columns), BF16)],
        1_000_000, mine, got_x,
        scratch=[pltpu.VMEM((TOK, columns), F32)],
    )
    got_z = flip(send, 4)
    dq = query_grad(saved)
    (eighth,) = call(pair_sum_kernel, [((128, columns), BF16)], 1_000_000, kept, got_z)
    eighths = lax.all_to_all(eighth.reshape(8, 16, -1), ("z2", "z1", "x1"), 0, 0)
    keep, give = call(head_sum_kernel, [((8, LATENT + ROPE), F32)] * 2, 1_000_000, parts)
    grad_compressed = keep + ctx_shift(give, -1)
    grad_weight = jnp.sum(eighths.astype(F32), axis=0)
    return dq, grad_compressed, grad_weight


def solution(mesh):
    fine = Mesh(mesh.devices.reshape(2, 2, 2, 2, 2, 2, 8, 2), CTX + HEAD)
    placed = (P(CTX, None), P(CTX, HEAD), P(CTX, HEAD), P(None, HEAD), P())
    return jax.shard_map(
        body,
        mesh=fine,
        in_specs=placed,
        out_specs=(P(CTX, HEAD), P(CTX + HEAD, None), P(CTX, HEAD)),
        check_vma=False,
    )
```
